32 devices in a mesh: feat: 2 (over x), lat: 16 (over z, y, core).
Axes of the slice: x: 2, y: 2, z: 4, core: 2. Of those that a mesh axis runs over, the one named last changes fastest.
Arguments:
- acts: bfloat16 [2, 128, 4096], P(None, 'lat', 'feat'), may hold values from -6 to 6
- weight: bfloat16 [2, 4096, 16384], P(None, 'feat', 'lat'), may hold values from -0.0625 to 0.0625
- enc_bias: float32 [16384], P('lat'), may hold values from -1 to 0.5
- dec_bias: float32 [2, 4096], P(None, 'feat'), may hold values from -1 to 1
Outputs:
- grad_weight: bfloat16 [2, 4096, 16384], P(None, 'feat', 'lat')
- grad_enc_bias: float32 [16384], P('lat')
- grad_dec_bias: float32 [2, 4096], P(None, 'feat')
The draws below stay inside these ranges and needn't reach their ends.
All inputs are finite; a program needn't handle non-finite values.
Results may differ from the reference program's by a relative error of at most 0.0085.
Values may be sent and summed in bfloat16 or wider, within the bound.
No kernel may reach another device: no remote copies, remote signals or barrier semaphores. Data moves between devices by JAX's collectives and lax.ppermute only.
A program may use at most 128 MiB of HBM per device.

```python
import math
import jax
import jax.numpy as jnp
from jax import lax

D = 4096
LAT_DEV = 1024
LATENTS = 16384
ROWS = 128
N_FEAT = 2
N_LAT = 16


def block_levels(key, extent, split, least, largest):
    loudness, own = 1.0, jax.random.fold_in(key, 6)
    for axis_at, blocks in split:
        heights = jnp.exp(jax.random.uniform(jax.random.fold_in(own, axis_at), (blocks,), jnp.float32, least / len(split), largest / len(split)))
        loudness = loudness * jnp.repeat(heights, extent[axis_at] // blocks).reshape([-1 if axis == axis_at else 1 for axis in range(len(extent))])
    return loudness


def bell_draw(key, extent, deviation, limit, cuts=(), kind=jnp.bfloat16):
    gain = block_levels(key, extent, cuts, -0.22, 0.18) if cuts else 1.0
    drawn = jax.random.normal(key, extent, jnp.float32) * deviation * gain
    return jnp.minimum(jnp.maximum(drawn, -limit), limit).astype(kind)


def setup_inputs(seed: int = 0) -> dict:
    key_of = jax.random.split(jax.random.key(seed), 5)
    return {
        "acts": bell_draw(key_of[0], (2, ROWS, D), 1.0, 6.0, ((1, 16), (2, 2))),
        "weight": bell_draw(key_of[1], (2, D, LATENTS), (2 * D) ** -0.5, 0.0625, ((1, 2), (2, 16))),
        "enc_bias": jnp.clip(-1.0 + 1.5 * jax.random.uniform(key_of[2], (LATENTS,), jnp.float32) ** block_levels(key_of[2], (LATENTS,), ((0, 16),), -0.2, 0.2), -1.0, 0.5),
        "dec_bias": jnp.clip(jax.random.uniform(key_of[3], (2, D), jnp.float32, -1.0, 1.0) * block_levels(key_of[3], (2, D), ((1, 2),), -0.4, 0.0), -1.0, 1.0),
    }


def grouped(left, right):
    part = left.shape[2] // N_FEAT
    total = jnp.zeros((left.shape[1], right.shape[2]), jnp.float32)
    for group in range(N_FEAT):
        low = group * part
        term = jnp.dot(left[0, :, low:low + part], right[0, low:low + part, :], preferred_element_type=jnp.float32)
        term = term + jnp.dot(left[1, :, low:low + part], right[1, low:low + part, :], preferred_element_type=jnp.float32)
        rounded = lax.optimization_barrier(term.astype(jnp.bfloat16))
        total = total + rounded.astype(jnp.float32)
    return total

def reference(acts, weight, enc_bias, dec_bias):
    width = acts.shape[2]
    lats = weight.shape[2]
    scale = math.sqrt(2.0 * width / lats)
    starts = jnp.arange(N_LAT, dtype=jnp.int32) * LAT_DEV

    def forward(carry, start):
        block = lax.dynamic_slice_in_dim(weight, start, LAT_DEV, 2)
        bias_block = lax.dynamic_slice_in_dim(enc_bias, start, LAT_DEV, 0)
        pre = grouped(acts, block) + bias_block
        latents = jax.nn.softplus(pre).astype(jnp.bfloat16)
        first = jnp.dot(latents, block[0].T, preferred_element_type=jnp.float32)
        second = jnp.dot(latents, block[1].T, preferred_element_type=jnp.float32)
        return (carry + jnp.stack([first, second]), pre)
    zeros = jnp.zeros((2, acts.shape[1], width), jnp.float32)
    summed, pres = lax.scan(forward, zeros, starts)
    resid = scale * summed + dec_bias[:, None, :] - acts.astype(jnp.float32)
    grad_dec_bias = lax.optimization_barrier(jnp.sum(resid, axis=1))
    resid_b = resid.astype(jnp.bfloat16)

    def backward(carry, inputs):
        start, pre = inputs
        block = lax.dynamic_slice_in_dim(weight, start, LAT_DEV, 2)
        latents = jax.nn.softplus(pre).astype(jnp.bfloat16)
        grad_pre = scale * grouped(resid_b, block) * jax.nn.sigmoid(pre)
        bias_part = lax.optimization_barrier(jnp.sum(grad_pre, axis=0))
        grad_pre_b = grad_pre.astype(jnp.bfloat16)
        outs = []
        for model in range(2):
            enc_term = jnp.dot(acts[model].T, grad_pre_b, preferred_element_type=jnp.float32)
            dec_term = jnp.dot(resid_b[model].T, latents, preferred_element_type=jnp.float32)
            outs.append((enc_term + scale * dec_term).astype(jnp.bfloat16))
        return (carry, (jnp.stack(outs), bias_part))
    unused, (blocks, bias_blocks) = lax.scan(backward, jnp.zeros((), jnp.float32), (starts, pres))
    grad_weight = jnp.transpose(blocks, (1, 2, 0, 3)).reshape(2, width, lats)
    grad_enc_bias = bias_blocks.reshape(lats)
    return (grad_weight, grad_enc_bias, grad_dec_bias)
```

```python
import functools
import math

import jax
import jax.numpy as jnp
from jax import lax
from jax.experimental import pallas as pl
from jax.experimental.pallas import tpu as pltpu
from jax.sharding import PartitionSpec as P

F32 = jnp.float32
BF16 = jnp.bfloat16


def radices(size):
    stages, stride = [], 1
    while size > 1:
        if stride == 1 or size == 8:
            radix = 2
        else:
            radix = 4
        if size % radix:
            radix = size
        stages.append((stride, radix))
        stride *= radix
        size //= radix
    return stages[::-1]


def shift(x, size, stride, radix, step):
    pairs = []
    for dst in range(size):
        digit = dst // stride % radix
        src = dst + ((digit + step) % radix - digit) * stride
        pairs.append((src, dst))
    return lax.ppermute(x, "lat", pairs)


def gather_rows(x, size):
    for stride, radix in radices(size):
        others = [shift(x, size, stride, radix, step) for step in range(1, radix)]
        x = jnp.concatenate([x] + others, axis=1)
    return x


def scatter_sum(x, size):
    for stride, radix in radices(size)[::-1]:
        rows = x.shape[1] // radix
        parts = [x[:, k * rows:(k + 1) * rows] for k in range(radix)]
        x = parts[0].astype(F32)
        for step in range(1, radix):
            sent = parts[radix - step].astype(BF16)
            x = x + shift(sent, size, stride, radix, step).astype(F32)
    return x


def feat_others(x, n_feat):
    got = []
    for step in range(1, n_feat):
        pairs = [((d + step) % n_feat, d) for d in range(n_feat)]
        got.append(lax.ppermute(x, "feat", pairs))
    return got


def add_terms(own, others):
    total = own.astype(F32)
    for other in others:
        total = total + other.astype(F32)
    return total


def times_weight_kernel(left_ref, weight_ref, out_ref, acc_ref):
    step = pl.program_id(0) * pl.num_programs(1) + pl.program_id(1)
    term = jnp.dot(left_ref[0], weight_ref[0], preferred_element_type=F32)

    @pl.when(step == 0)
    def _():
        acc_ref[...] = term

    @pl.when(step > 0)
    def _():
        acc_ref[...] += term

    @pl.when(step == pl.num_programs(0) * pl.num_programs(1) - 1)
    def _():
        out_ref[...] = acc_ref[...].astype(out_ref.dtype)


def times_weight(left, weight):
    models, rows, width = left.shape
    lats = weight.shape[2]
    block = min(width, 512)
    return pl.pallas_call(
        times_weight_kernel,
        out_shape=jax.ShapeDtypeStruct((rows, lats), BF16),
        grid=(models, width // block),
        in_specs=[
            pl.BlockSpec((1, rows, block), lambda m, k: (m, 0, k)),
            pl.BlockSpec((1, block, lats), lambda m, k: (m, k, 0)),
        ],
        out_specs=pl.BlockSpec((rows, lats), lambda m, k: (0, 0)),
        scratch_shapes=[pltpu.VMEM((rows, lats), F32)],
        compiler_params=pltpu.CompilerParams(vmem_limit_bytes=24 << 20),
        cost_estimate=pl.CostEstimate(
            flops=2 * models * rows * width * lats,
            bytes_accessed=2 * models * width * lats,
            transcendentals=0,
        ),
    )(left, weight)


def decode_kernel(lat_ref, weight_ref, out_ref):
    out_ref[0] = lax.dot_general(
        lat_ref[...], weight_ref[0], (((1,), (1,)), ((), ())), preferred_element_type=F32
    ).astype(out_ref.dtype)


def decode(latents, weight):
    models, width, lats = weight.shape
    rows = latents.shape[0]
    block = min(width, 512)
    return pl.pallas_call(
        decode_kernel,
        out_shape=jax.ShapeDtypeStruct((models, rows, width), BF16),
        grid=(models, width // block),
        in_specs=[
            pl.BlockSpec((rows, lats), lambda m, k: (0, 0)),
            pl.BlockSpec((1, block, lats), lambda m, k: (m, k, 0)),
        ],
        out_specs=pl.BlockSpec((1, rows, block), lambda m, k: (m, 0, k)),
        compiler_params=pltpu.CompilerParams(vmem_limit_bytes=24 << 20),
        cost_estimate=pl.CostEstimate(
            flops=2 * models * rows * width * lats,
            bytes_accessed=2 * models * width * lats,
            transcendentals=0,
        ),
    )(latents, weight)


def grad_kernel(scale, acts_ref, resid_ref, grad_ref, lat_ref, out_ref):
    contract = (((0,), (0,)), ((), ()))
    left = jnp.concatenate([acts_ref[0], resid_ref[0]], axis=0)
    right = jnp.concatenate([grad_ref[...], lat_ref[...]], axis=0)
    total = lax.dot_general(left, right, contract, preferred_element_type=F32)
    out_ref[0] = (scale * total).astype(out_ref.dtype)


def grad_weights(scale, acts, resid, grad, latents):
    models, rows, width = acts.shape
    lats = latents.shape[1]
    block = min(width, 512)
    side = pl.BlockSpec((1, rows, block), lambda m, k: (m, 0, k))
    whole = pl.BlockSpec((rows, lats), lambda m, k: (0, 0))
    return pl.pallas_call(
        functools.partial(grad_kernel, scale),
        out_shape=jax.ShapeDtypeStruct((models, width, lats), BF16),
        grid=(models, width // block),
        in_specs=[side, side, whole, whole],
        out_specs=pl.BlockSpec((1, block, lats), lambda m, k: (m, k, 0)),
        compiler_params=pltpu.CompilerParams(vmem_limit_bytes=32 << 20),
        cost_estimate=pl.CostEstimate(
            flops=4 * models * rows * width * lats,
            bytes_accessed=2 * models * width * lats,
            transcendentals=0,
        ),
    )(acts, resid, grad, latents)


def on_device(acts, weight, enc_bias, dec_bias):
    n_feat, n_lat = lax.axis_size("feat"), lax.axis_size("lat")
    scale = math.sqrt(2.0 * weight.shape[1] * n_feat / (weight.shape[2] * n_lat))
    whole = gather_rows(acts, n_lat)
    own = times_weight(whole, weight)
    pre = add_terms(own, feat_others(own, n_feat)) + enc_bias
    latents = jax.nn.softplus(pre).astype(BF16)
    recon = scatter_sum(decode(latents, weight), n_lat)
    resid = (scale * recon + dec_bias[:, None, :] - acts.astype(F32)).astype(BF16)
    resid_rows = gather_rows(resid, n_lat)
    grad_dec_bias = jnp.sum(resid_rows.astype(F32), axis=1)
    back = times_weight(resid_rows, weight)
    grad_pre = add_terms(back, feat_others(back, n_feat)) * jax.nn.sigmoid(pre)
    grad_enc_bias = scale * jnp.sum(grad_pre, axis=0)
    grad_weight = grad_weights(scale, whole, resid_rows, grad_pre.astype(BF16), latents)
    return (grad_weight, grad_enc_bias, grad_dec_bias)


def solution(mesh):
    placed = (P(None, "lat", "feat"), P(None, "feat", "lat"), P("lat"), P(None, "feat"))
    return jax.shard_map(
        on_device,
        mesh=mesh,
        in_specs=placed,
        out_specs=(P(None, "feat", "lat"), P("lat"), P(None, "feat")),
        check_vma=False,
    )
```

```python
import functools
import math

import jax
import jax.numpy as jnp
from jax import lax
from jax.experimental import pallas as pl
from jax.experimental.pallas import tpu as pltpu
from jax.sharding import PartitionSpec as P

F32 = jnp.float32
BF16 = jnp.bfloat16
WHOLE = pl.BlockSpec(memory_space=pltpu.VMEM)
MIB = 1 << 20


def stages(size):
    found, stride = [], 1
    while size > 1:
        radix = 2 if stride == 1 or size == 8 else 4
        if size % radix:
            radix = size
        found.append((stride, radix))
        stride *= radix
        size //= radix
    while len(found) < 2:
        found.append((stride, 1))
    return found[0], found[1], found[2:]


def shift(x, size, stage, step):
    stride, radix = stage
    pairs = []
    for dst in range(size):
        digit = dst // stride % radix
        pairs.append((dst + ((digit + step) % radix - digit) * stride, dst))
    return lax.ppermute(x, "lat", pairs)


def feat_others(x, n_feat):
    got = []
    for step in range(1, n_feat):
        pairs = [((d + step) % n_feat, d) for d in range(n_feat)]
        got.append(lax.ppermute(x, "feat", pairs))
    return got


def add_terms(own, others):
    total = own.astype(F32)
    for other in others:
        total = total + other.astype(F32)
    return total


def call(kernel, outs, args, flops=0, moved=0, limit=20 * MIB, **kwargs):
    return pl.pallas_call(
        kernel,
        out_shape=outs,
        compiler_params=pltpu.CompilerParams(vmem_limit_bytes=limit),
        cost_estimate=pl.CostEstimate(flops=flops, bytes_accessed=moved, transcendentals=0),
        **kwargs,
    )(*args)


def load_kernel(parts, weight_ref, out_ref, sems):
    models, width, _ = weight_ref.shape
    rows = width // parts
    copies = []
    for m in range(models):
        for k in range(parts):
            here = pl.ds(k * rows, rows)
            copies.append(
                pltpu.make_async_copy(
                    weight_ref.at[m, here], out_ref.at[m, here], sems.at[m * parts + k]
                )
            )
    for copy in copies:
        copy.start()
    for copy in copies:
        copy.wait()


def load_weight(weight):
    parts = 4
    return call(
        functools.partial(load_kernel, parts),
        jax.ShapeDtypeStruct(weight.shape, weight.dtype),
        (weight,),
        moved=4 * weight.size,
        in_specs=[pl.BlockSpec(memory_space=pltpu.HBM)],
        out_specs=WHOLE,
        scratch_shapes=[pltpu.SemaphoreType.DMA((weight.shape[0] * parts,))],
        name="load_weight",
    )


def times_kernel(*refs):
    lefts, weight_ref, out_ref = refs[:-2], refs[-2], refs[-1]
    total = None
    for m in range(weight_ref.shape[0]):
        left = jnp.concatenate([ref[m] for ref in lefts], axis=0)
        term = jnp.dot(left, weight_ref[m], preferred_element_type=F32)
        total = term if total is None else total + term
    out_ref[...] = total.astype(out_ref.dtype)


def times_weight(lefts, weight):
    models, width, lats = weight.shape
    rows = sum(left.shape[1] for left in lefts)
    return call(
        times_kernel,
        jax.ShapeDtypeStruct((rows, lats), BF16),
        (*lefts, weight),
        flops=2 * models * rows * width * lats,
        moved=2 * rows * lats,
        in_specs=[WHOLE] * (len(lefts) + 1),
        out_specs=WHOLE,
        name="times_weight",
    )


def decode_kernel(lat_ref, weight_ref, keep_ref, *send_refs):
    models, width, _ = weight_ref.shape
    rows = keep_ref.shape[1]
    block = min(width, 512)
    for m in range(models):
        for k in range(width // block):
            cols = slice(k * block, (k + 1) * block)
            term = lax.dot_general(
                lat_ref[...],
                weight_ref[m, cols, :],
                (((1,), (1,)), ((), ())),
                preferred_element_type=F32,
            )
            keep_ref[m, :, cols] = term[:rows]
            for p, ref in enumerate(send_refs):
                ref[m, :, cols] = term[(p + 1) * rows:(p + 2) * rows].astype(BF16)


def decode(latents, weight, cores):
    models, width, lats = weight.shape
    rows = latents.shape[0] // cores
    piece = (models, rows, width)
    return call(
        decode_kernel,
        (jax.ShapeDtypeStruct(piece, F32),) + (jax.ShapeDtypeStruct(piece, BF16),) * (cores - 1),
        (latents, weight),
        flops=2 * models * rows * cores * width * lats,
        moved=4 * models * rows * cores * width,
        in_specs=[WHOLE] * 2,
        out_specs=(WHOLE,) * cores,
        name="decode",
    )


def turn_kernel(*refs):
    out_ref = refs[-1]
    models, width, _ = out_ref.shape
    block = min(width, 512)
    for m in range(models):
        for k in range(width // block):
            cols = slice(k * block, (k + 1) * block)
            rows = jnp.concatenate([ref[m, :, cols] for ref in refs[:-1]], axis=0)
            out_ref[m, cols, :] = rows.T


def turn(lefts):
    models, _, width = lefts[0].shape
    rows = sum(left.shape[1] for left in lefts)
    return call(
        turn_kernel,
        jax.ShapeDtypeStruct((models, width, rows), BF16),
        lefts,
        moved=4 * models * width * rows,
        in_specs=[WHOLE] * len(lefts),
        out_specs=WHOLE,
        name="turn",
    )


def grad_kernel(scale, groups, *refs):
    acts_ref, resid_ref = refs[:2]
    own, others = refs[2:2 + groups], refs[2 + groups:2 + 2 * groups]
    slopes, lats = refs[2 + 2 * groups:2 + 3 * groups], refs[2 + 3 * groups:2 + 4 * groups]
    out_ref, bias_ref, right_ref = refs[2 + 4 * groups:]

    @pl.when((pl.program_id(0) == 0) & (pl.program_id(1) == 0))
    def _():
        bias, low = None, 0
        for own_ref, other_ref, slope_ref in zip(own, others, slopes):
            rows = own_ref.shape[0]
            grad = own_ref[...].astype(F32)
            for k in range(other_ref.shape[0]):
                grad = grad + other_ref[k].astype(F32)
            grad = grad * slope_ref[...]
            part = jnp.sum(grad, axis=0, keepdims=True)
            bias = part if bias is None else bias + part
            right_ref[low:low + rows, :] = grad.astype(BF16)
            low += rows
        for ref in lats:
            right_ref[low:low + ref.shape[0], :] = ref[...]
            low += ref.shape[0]
        bias_ref[...] = scale * bias

    left = jnp.concatenate([acts_ref[0], resid_ref[0]], axis=1)
    total = jnp.dot(left, right_ref[...], preferred_element_type=F32)
    out_ref[0] = (scale * total).astype(out_ref.dtype)


def grad_weights(scale, acts, resid, own, others, slopes, latents):
    models, width, rows = acts.shape
    lats = latents[0].shape[1]
    block = min(width, 512)
    groups = len(own)
    side = pl.BlockSpec((1, block, rows), lambda m, k: (m, k, 0))
    flat = [pl.BlockSpec(x.shape, lambda m, k: (0, 0)) for x in own]
    deep = [pl.BlockSpec(x.shape, lambda m, k: (0, 0, 0)) for x in others]
    return call(
        functools.partial(grad_kernel, scale, groups),
        (
            jax.ShapeDtypeStruct((models, width, lats), BF16),
            jax.ShapeDtypeStruct((1, lats), F32),
        ),
        (acts, resid, *own, *others, *slopes, *latents),
        flops=4 * models * rows * width * lats,
        moved=2 * models * width * lats,
        limit=24 * MIB,
        grid=(models, width // block),
        in_specs=[side, side] + flat + deep + flat + flat,
        out_specs=(
            pl.BlockSpec((1, block, lats), lambda m, k: (m, k, 0)),
            pl.BlockSpec((1, lats), lambda m, k: (0, 0)),
        ),
        scratch_shapes=[pltpu.VMEM((2 * rows, lats), BF16)],
        name="grad_weights",
    )


def gather_groups(x, size):
    core, group, rest = stages(size)
    early = [shift(x, size, group, step) for step in range(1, group[1])]
    block = x
    late = []
    for stage in rest[::-1]:
        others = [shift(block, size, stage, step) for step in range(1, stage[1])]
        block = jnp.concatenate([block] + others, axis=1)
    tail = block[:, x.shape[1]:]
    blocks = [block]
    for step in range(1, group[1]):
        moved = shift(tail, size, group, step)
        blocks.append(jnp.concatenate([early[step - 1], moved], axis=1))
    return [
        [b] + [shift(b, size, core, step) for step in range(1, core[1])] for b in blocks
    ]


def sum_group(keep, sends, size):
    core, _, rest = stages(size)
    total = keep
    for step in range(1, core[1]):
        total = total + shift(sends[core[1] - step - 1], size, core, step).astype(F32)
    for stage in rest:
        radix = stage[1]
        rows = total.shape[1] // radix
        parts = [total[:, k * rows:(k + 1) * rows] for k in range(radix)]
        total = parts[0]
        for step in range(1, radix):
            sent = parts[radix - step].astype(BF16)
            total = total + shift(sent, size, stage, step).astype(F32)
    return total


def on_device(acts, weight, enc_bias, dec_bias):
    n_feat, n_lat = lax.axis_size("feat"), lax.axis_size("lat")
    core, group, _ = stages(n_lat)
    n_group = group[1]
    scale = math.sqrt(2.0 * weight.shape[1] * n_feat / (weight.shape[2] * n_lat))
    held = load_weight(weight)
    whole = gather_groups(acts, n_lat)
    own = [times_weight(pieces, held) for pieces in whole]
    got = [feat_others(x, n_feat) for x in own]
    pre = [add_terms(x, y) + enc_bias for x, y in zip(own, got)]
    latents = [jax.nn.softplus(x).astype(BF16) for x in pre]
    slopes = [jax.nn.sigmoid(x) for x in pre]
    sums = []
    for x in latents:
        keep, *sends = decode(x, held, core[1])
        sums.append(sum_group(keep, sends, n_lat))
    recon = sums[0]
    for step in range(1, n_group):
        sent = sums[n_group - step].astype(BF16)
        recon = recon + shift(sent, n_lat, group, step).astype(F32)
    resid = (scale * recon + dec_bias[:, None, :] - acts.astype(F32)).astype(BF16)
    resid_rows = gather_groups(resid, n_lat)
    back = [times_weight(pieces, held) for pieces in resid_rows]
    others = [jnp.stack(feat_others(x, n_feat)) for x in back]
    flat_acts = [x for pieces in whole for x in pieces]
    flat_resid = [x for pieces in resid_rows for x in pieces]
    grad_dec_bias = sum(jnp.sum(x.astype(F32), axis=1) for x in flat_resid)
    grad_weight, grad_enc_bias = grad_weights(
        scale, turn(flat_acts), turn(flat_resid), back, others, slopes, latents
    )
    return (grad_weight, grad_enc_bias.reshape(-1), grad_dec_bias)


def solution(mesh):
    placed = (P(None, "lat", "feat"), P(None, "feat", "lat"), P("lat"), P(None, "feat"))
    return jax.shard_map(
        on_device,
        mesh=mesh,
        in_specs=placed,
        out_specs=(P(None, "feat", "lat"), P("lat"), P(None, "feat")),
        check_vma=False,
    )
```

```python
import functools
import math

import jax
import jax.numpy as jnp
from jax import lax
from jax.experimental import pallas as pl
from jax.experimental.pallas import tpu as pltpu
from jax.sharding import PartitionSpec as P


F32 = jnp.float32
BF16 = jnp.bfloat16
WHOLE = pl.BlockSpec(memory_space=pltpu.VMEM)
MIB = 1 << 20


def stages(size):
    found, stride = [], 1
    while size > 1:
        radix = 2 if stride == 1 or size == 8 else 4
        if size % radix:
            radix = size
        found.append((stride, radix))
        stride *= radix
        size //= radix
    while len(found) < 2:
        found.append((stride, 1))
    return found[0], found[1], found[2:]


def shift(x, size, stage, step):
    stride, radix = stage
    if radix & (radix - 1):
        raise ValueError("radix")
    pairs = []
    for dst in range(size):
        digit = dst // stride % radix
        pairs.append((dst + ((digit ^ step) - digit) * stride, dst))
    return lax.ppermute(x, "lat", pairs)


def feat_others(x, n_feat):
    got = []
    for step in range(1, n_feat):
        pairs = [((d + step) % n_feat, d) for d in range(n_feat)]
        got.append(lax.ppermute(x, "feat", pairs))
    return got


def add_terms(own, others):
    total = own.astype(F32)
    for other in others:
        total = total + other.astype(F32)
    return total


def call(kernel, outs, args, flops=0, moved=0, limit=20 * MIB, **kwargs):
    return pl.pallas_call(
        kernel,
        out_shape=outs,
        compiler_params=pltpu.CompilerParams(vmem_limit_bytes=limit),
        cost_estimate=pl.CostEstimate(flops=flops, bytes_accessed=moved, transcendentals=0),
        **kwargs,
    )(*args)


def load_kernel(m, parts, weight_ref, out_ref, sems):
    rows = out_ref.shape[0] // parts
    copies = []
    for k in range(parts):
        here = pl.ds(k * rows, rows)
        copies.append(
            pltpu.make_async_copy(weight_ref.at[m, here], out_ref.at[here], sems.at[k])
        )
    for copy in copies:
        copy.start()
    for copy in copies:
        copy.wait()


def load_weight(weight, m):
    parts = 4
    return call(
        functools.partial(load_kernel, m, parts),
        jax.ShapeDtypeStruct(weight.shape[1:], weight.dtype),
        (weight,),
        moved=2 * weight.size,
        limit=44 * MIB,
        in_specs=[pl.BlockSpec(memory_space=pltpu.HBM)],
        out_specs=WHOLE,
        scratch_shapes=[pltpu.SemaphoreType.DMA((parts,))],
        name="load_weight",
    )


def times_kernel(models, *refs):
    lefts, weights, out_ref = refs[:-models - 1], refs[-models - 1:-1], refs[-1]
    total = None
    for m in range(models):
        left = jnp.concatenate([ref[m] for ref in lefts], axis=0)
        term = jnp.dot(left, weights[m][...], preferred_element_type=F32)
        total = term if total is None else total + term
    out_ref[...] = total.astype(out_ref.dtype)


def times_weight(lefts, weights):
    width, lats = weights[0].shape
    rows = sum(left.shape[1] for left in lefts)
    return call(
        functools.partial(times_kernel, len(weights)),
        jax.ShapeDtypeStruct((rows, lats), BF16),
        (*lefts, *weights),
        flops=2 * len(weights) * rows * width * lats,
        moved=2 * rows * lats,
        in_specs=[WHOLE] * (len(lefts) + len(weights)),
        out_specs=WHOLE,
        name="times_weight",
    )


def decode_kernel(cores, own_ref, bias_ref, turned_ref, *refs):
    others, lat_ref, keep_ref, sends = refs[:-cores - 1], refs[-cores - 1], refs[-cores], refs[len(refs) - cores + 1:]
    models, rows, width = keep_ref.shape
    pre = own_ref[...].astype(F32)
    for ref in others:
        pre = pre + ref[...].astype(F32)
    pre = pre + bias_ref[...]
    latents = jnp.maximum(pre, 0.0) + jnp.log1p(jnp.exp(-jnp.abs(pre)))
    latents = latents.astype(BF16)
    lat_ref[...] = latents
    block = min(width, 512)
    for m in range(models):
        for k in range(width // block):
            cols = slice(k * block, (k + 1) * block)
            term = jnp.dot(latents, turned_ref[m, :, cols], preferred_element_type=F32)
            keep_ref[m, :, cols] = term[:rows]
            for p, ref in enumerate(sends):
                ref[m, :, cols] = term[(p + 1) * rows:(p + 2) * rows].astype(BF16)


def decode(own, others, bias, turned, cores):
    models, lats, width = turned.shape
    rows = own.shape[0] // cores
    piece = (models, rows, width)
    return call(
        functools.partial(decode_kernel, cores),
        (jax.ShapeDtypeStruct(own.shape, BF16), jax.ShapeDtypeStruct(piece, F32))
        + (jax.ShapeDtypeStruct(piece, BF16),) * (cores - 1),
        (own, bias, turned, *others),
        flops=2 * models * rows * cores * width * lats,
        moved=4 * models * rows * cores * width,
        in_specs=[WHOLE] * (3 + len(others)),
        out_specs=(WHOLE,) * (cores + 1),
        name="decode",
    )


def turn_kernel(*refs):
    out_ref = refs[-1]
    models, width, _ = out_ref.shape
    block = min(width, 512)
    for m in range(models):
        for k in range(width // block):
            cols = slice(k * block, (k + 1) * block)
            rows = jnp.concatenate([ref[m, :, cols] for ref in refs[:-1]], axis=0)
            out_ref[m, cols, :] = rows.T


def turn(lefts):
    models, _, width = lefts[0].shape
    rows = sum(left.shape[1] for left in lefts)
    return call(
        turn_kernel,
        jax.ShapeDtypeStruct((models, width, rows), BF16),
        lefts,
        moved=4 * models * width * rows,
        in_specs=[WHOLE] * len(lefts),
        out_specs=WHOLE,
        name="turn",
    )


def turn_weight_kernel(*refs):
    out_ref = refs[-1]
    width = refs[0].shape[0]
    block = min(width, 512)
    for m, weight_ref in enumerate(refs[:-1]):
        for k in range(width // block):
            cols = slice(k * block, (k + 1) * block)
            out_ref[m, :, cols] = weight_ref[cols, :].T


def turn_weight(weights):
    width, lats = weights[0].shape
    models = len(weights)
    return call(
        turn_weight_kernel,
        jax.ShapeDtypeStruct((models, lats, width), BF16),
        tuple(weights),
        moved=4 * models * width * lats,
        in_specs=[WHOLE] * models,
        out_specs=WHOLE,
        name="turn_weight",
    )


def grad_kernel(scale, groups, slots, *refs):
    acts_ref, resid_ref = refs[:2]
    own, others = refs[2:2 + groups], refs[2 + groups:2 + 2 * groups]
    slopes, latents = refs[2 + 2 * groups:2 + 3 * groups], refs[2 + 3 * groups:2 + 4 * groups]
    out_ref, bias_ref, right_ref, held_ref, sems = refs[2 + 4 * groups:]
    bias, low = None, 0
    for own_ref, other_ref, slope_ref in zip(own, others, slopes):
        rows = own_ref.shape[0]
        grad = own_ref[...].astype(F32)
        for k in range(other_ref.shape[0]):
            grad = grad + other_ref[k].astype(F32)
        grad = grad * slope_ref[...]
        part = jnp.sum(grad, axis=0, keepdims=True)
        bias = part if bias is None else bias + part
        right_ref[low:low + rows, :] = grad.astype(BF16)
        low += rows
    for ref in latents:
        right_ref[low:low + ref.shape[0], :] = ref[...]
        low += ref.shape[0]
    bias_ref[...] = scale * bias
    models, width, _ = acts_ref.shape
    _, block, lats = held_ref.shape
    strip = min(lats, 256)
    places = [(m, k * block) for m in range(models) for k in range(width // block)]
    copies = []
    for i, (m, low) in enumerate(places):
        here = pl.ds(low, block)
        if i >= slots:
            copies[i - slots].wait()
        left = jnp.concatenate([acts_ref[m, here, :], resid_ref[m, here, :]], axis=1)
        for first in range(0, lats, strip):
            cols = slice(first, first + strip)
            total = jnp.dot(left, right_ref[:, cols], preferred_element_type=F32)
            held_ref[i % slots, :, cols] = (scale * total).astype(BF16)
        copies.append(
            pltpu.make_async_copy(held_ref.at[i % slots], out_ref.at[m, here], sems.at[i % slots])
        )
        copies[i].start()
    for copy in copies[-slots:]:
        copy.wait()


def grad_weights(scale, acts, resid, own, others, slopes, latents):
    models, width, rows = acts.shape
    lats = latents[0].shape[1]
    block = min(width, 512)
    groups, slots = len(own), 4
    return call(
        functools.partial(grad_kernel, scale, groups, slots),
        (
            jax.ShapeDtypeStruct((models, width, lats), BF16),
            jax.ShapeDtypeStruct((1, lats), F32),
        ),
        (acts, resid, *own, *others, *slopes, *latents),
        flops=4 * models * rows * width * lats,
        moved=2 * models * width * lats,
        in_specs=[WHOLE] * (2 + 4 * groups),
        out_specs=(pl.BlockSpec(memory_space=pltpu.HBM), WHOLE),
        scratch_shapes=[
            pltpu.VMEM((2 * rows, lats), BF16),
            pltpu.VMEM((slots, block, lats), BF16),
            pltpu.SemaphoreType.DMA((slots,)),
        ],
        name="grad_weights",
    )


def gather_groups(x, size, begin, work):
    core, group, rest = stages(size)
    early = [shift(x, size, group, step) for step in range(1, group[1])]
    block = x
    for stage in rest[::-1]:
        others = [shift(block, size, stage, step) for step in range(1, stage[1])]
        block = jnp.concatenate([block] + others, axis=1)
    tail = block[:, x.shape[1]:]
    tail = begin(tail)
    moved = [shift(tail, size, group, step) for step in range(1, group[1])]
    pieces, done = [], []
    for k in range(group[1]):
        if k:
            rest_rows, done[k - 1] = lax.optimization_barrier((moved[k - 1], done[k - 1]))
            block = jnp.concatenate([early[k - 1], rest_rows], axis=1)
        piece = [block] + [shift(block, size, core, step) for step in range(1, core[1])]
        pieces.append(piece)
        done.append(work(piece))
    return pieces, done


def sum_group(keep, sends, size):
    core, _, rest = stages(size)
    total = keep
    for step in range(1, core[1]):
        total = total + shift(sends[step - 1], size, core, step).astype(F32)
    for stage in rest:
        radix = stage[1]
        rows = total.shape[1] // radix
        parts = [total[:, k * rows:(k + 1) * rows] for k in range(radix)]
        total = parts[0]
        for step in range(1, radix):
            sent = parts[step].astype(BF16)
            total = total + shift(sent, size, stage, step).astype(F32)
    return total


def on_device(acts, weight, enc_bias, dec_bias):
    n_feat, n_lat = lax.axis_size("feat"), lax.axis_size("lat")
    core, group, _ = stages(n_lat)
    n_group = group[1]
    scale = math.sqrt(2.0 * weight.shape[1] * n_feat / (weight.shape[2] * n_lat))
    held = [load_weight(weight, 0)]

    def begin(tail):
        gated, tail = lax.optimization_barrier((weight, tail))
        held.extend(load_weight(gated, m) for m in range(1, weight.shape[0]))
        return tail

    whole, own = gather_groups(acts, n_lat, begin, lambda x: times_weight(x, held))
    turned = turn_weight(held)
    got = []
    for x in own:
        got.append(feat_others(x, n_feat))
    latents, sums = [], []
    for x, others in zip(own, got):
        lat, keep, *sends = decode(x, others, enc_bias[None, :], turned, core[1])
        latents.append(lat)
        sums.append(sum_group(keep, sends, n_lat))
    slopes = [jax.nn.sigmoid(add_terms(x, y) + enc_bias) for x, y in zip(own, got)]
    recon = sums[0]
    for step in range(1, n_group):
        sent = sums[step].astype(BF16)
        recon = recon + shift(sent, n_lat, group, step).astype(F32)
    resid = (scale * recon + dec_bias[:, None, :] - acts.astype(F32)).astype(BF16)
    resid_rows, back = gather_groups(resid, n_lat, lambda x: x, lambda x: times_weight(x, held))
    others = [jnp.stack(feat_others(x, n_feat)) for x in back]
    flat_acts = [x for pieces in whole for x in pieces]
    flat_resid = [x for pieces in resid_rows for x in pieces]
    grad_dec_bias = sum(jnp.sum(x.astype(F32), axis=1) for x in flat_resid)
    grad_weight, grad_enc_bias = grad_weights(
        scale, turn(flat_acts), turn(flat_resid), back, others, slopes, latents
    )
    return (grad_weight, grad_enc_bias.reshape(-1), grad_dec_bias)


def solution(mesh):
    placed = (P(None, "lat", "feat"), P(None, "feat", "lat"), P("lat"), P(None, "feat"))
    return jax.shard_map(
        on_device,
        mesh=mesh,
        in_specs=placed,
        out_specs=(P(None, "feat", "lat"), P("lat"), P(None, "feat")),
        check_vma=False,
    )
```

```python
import functools
import math

import jax
import jax.numpy as jnp
from jax import lax
from jax.experimental import pallas as pl
from jax.experimental.pallas import tpu as pltpu
from jax.sharding import PartitionSpec as P


F32 = jnp.float32
BF16 = jnp.bfloat16
WHOLE = pl.BlockSpec(memory_space=pltpu.VMEM)
MIB = 1 << 20
HOLD_FLOPS = 1 << 33


def stages(size):
    found, stride = [], 1
    while size > 1:
        radix = 2 if stride == 1 or size == 8 else 4
        if size % radix:
            radix = size
        found.append((stride, radix))
        stride *= radix
        size //= radix
    while len(found) < 2:
        found.append((stride, 1))
    return found[0], found[1], found[2:]


def shift(x, size, stage, step):
    stride, radix = stage
    if radix & (radix - 1):
        raise ValueError("radix")
    pairs = []
    for dst in range(size):
        digit = dst // stride % radix
        pairs.append((dst + ((digit ^ step) - digit) * stride, dst))
    return lax.ppermute(x, "lat", pairs)


def feat_others(x, n_feat):
    got = []
    for step in range(1, n_feat):
        pairs = [((d + step) % n_feat, d) for d in range(n_feat)]
        got.append(lax.ppermute(x, "feat", pairs))
    return got


def add_terms(own, others):
    total = own.astype(F32)
    for other in others:
        total = total + other.astype(F32)
    return total


def call(kernel, outs, args, flops=0, moved=0, limit=20 * MIB, **kwargs):
    return pl.pallas_call(
        kernel,
        out_shape=outs,
        compiler_params=pltpu.CompilerParams(vmem_limit_bytes=limit),
        cost_estimate=pl.CostEstimate(flops=flops, bytes_accessed=moved, transcendentals=0),
        **kwargs,
    )(*args)


def hold_kernel(x_ref, out_ref):
    out_ref[...] = x_ref[...]


def hold(x):
    return call(
        hold_kernel,
        jax.ShapeDtypeStruct(x.shape, x.dtype),
        (x,),
        flops=HOLD_FLOPS,
        moved=4 * x.size,
        in_specs=[WHOLE],
        out_specs=WHOLE,
        name="hold",
    )


def times_kernel(*refs):
    lefts, weight_ref, out_ref = refs[:-2], refs[-2], refs[-1]
    total = None
    for m in range(weight_ref.shape[0]):
        left = jnp.concatenate([ref[m] for ref in lefts], axis=0)
        term = jnp.dot(left, weight_ref[m], preferred_element_type=F32)
        total = term if total is None else total + term
    out_ref[...] = total.astype(out_ref.dtype)


def times_weight(lefts, weight):
    models, width, lats = weight.shape
    rows = sum(left.shape[1] for left in lefts)
    return call(
        times_kernel,
        jax.ShapeDtypeStruct((rows, lats), BF16),
        (*lefts, weight),
        flops=2 * models * rows * width * lats,
        moved=2 * rows * lats,
        in_specs=[WHOLE] * (len(lefts) + 1),
        out_specs=WHOLE,
        name="times_weight",
    )


def decode_kernel(cores, own_ref, bias_ref, turned_ref, *refs):
    others, lat_ref, keep_ref, sends = refs[:-cores - 1], refs[-cores - 1], refs[-cores], refs[len(refs) - cores + 1:]
    models, rows, width = keep_ref.shape
    pre = own_ref[...].astype(F32)
    for ref in others:
        pre = pre + ref[...].astype(F32)
    pre = pre + bias_ref[...]
    latents = jnp.maximum(pre, 0.0) + jnp.log1p(jnp.exp(-jnp.abs(pre)))
    latents = latents.astype(BF16)
    lat_ref[...] = latents
    block = min(width, 512)
    for m in range(models):
        for k in range(width // block):
            cols = slice(k * block, (k + 1) * block)
            term = jnp.dot(latents, turned_ref[m, :, cols], preferred_element_type=F32)
            keep_ref[m, :, cols] = term[:rows]
            for p, ref in enumerate(sends):
                ref[m, :, cols] = term[(p + 1) * rows:(p + 2) * rows].astype(BF16)


def decode(own, others, bias, turned, cores):
    models, lats, width = turned.shape
    rows = own.shape[0] // cores
    piece = (models, rows, width)
    return call(
        functools.partial(decode_kernel, cores),
        (jax.ShapeDtypeStruct(own.shape, BF16), jax.ShapeDtypeStruct(piece, F32))
        + (jax.ShapeDtypeStruct(piece, BF16),) * (cores - 1),
        (own, bias, turned, *others),
        flops=2 * models * rows * cores * width * lats,
        moved=4 * models * rows * cores * width,
        in_specs=[WHOLE] * (3 + len(others)),
        out_specs=(WHOLE,) * (cores + 1),
        name="decode",
    )


def turn_kernel(*refs):
    out_ref = refs[-1]
    models, width, _ = out_ref.shape
    block = min(width, 512)
    for m in range(models):
        for k in range(width // block):
            cols = slice(k * block, (k + 1) * block)
            rows = jnp.concatenate([ref[m, :, cols] for ref in refs[:-1]], axis=0)
            out_ref[m, cols, :] = rows.T


def turn(lefts):
    models, _, width = lefts[0].shape
    rows = sum(left.shape[1] for left in lefts)
    return call(
        turn_kernel,
        jax.ShapeDtypeStruct((models, width, rows), BF16),
        lefts,
        moved=4 * models * width * rows,
        in_specs=[WHOLE] * len(lefts),
        out_specs=WHOLE,
        name="turn",
    )


def turn_weight_kernel(weight_ref, out_ref):
    models, width, _ = weight_ref.shape
    block = min(width, 512)
    for m in range(models):
        for k in range(width // block):
            cols = slice(k * block, (k + 1) * block)
            out_ref[m, :, cols] = weight_ref[m, cols, :].T


def turn_weight(weight):
    models, width, lats = weight.shape
    return call(
        turn_weight_kernel,
        jax.ShapeDtypeStruct((models, lats, width), weight.dtype),
        (weight,),
        moved=4 * weight.size,
        in_specs=[WHOLE],
        out_specs=WHOLE,
        name="turn_weight",
    )


def grad_kernel(scale, groups, slots, *refs):
    acts_ref, resid_ref = refs[:2]
    own, others = refs[2:2 + groups], refs[2 + groups:2 + 2 * groups]
    slopes, latents = refs[2 + 2 * groups:2 + 3 * groups], refs[2 + 3 * groups:2 + 4 * groups]
    out_ref, bias_ref, right_ref, held_ref, sems = refs[2 + 4 * groups:]
    bias, low = None, 0
    for own_ref, other_ref, slope_ref in zip(own, others, slopes):
        rows = own_ref.shape[0]
        grad = own_ref[...].astype(F32)
        for k in range(other_ref.shape[0]):
            grad = grad + other_ref[k].astype(F32)
        grad = grad * slope_ref[...]
        part = jnp.sum(grad, axis=0, keepdims=True)
        bias = part if bias is None else bias + part
        right_ref[low:low + rows, :] = grad.astype(BF16)
        low += rows
    for ref in latents:
        right_ref[low:low + ref.shape[0], :] = ref[...]
        low += ref.shape[0]
    bias_ref[...] = scale * bias
    models, width, _ = acts_ref.shape
    _, block, lats = held_ref.shape
    strip = min(lats, 256)
    places = [(m, k * block) for m in range(models) for k in range(width // block)]
    copies = []
    for i, (m, low) in enumerate(places):
        here = pl.ds(low, block)
        if i >= slots:
            copies[i - slots].wait()
        left = jnp.concatenate([acts_ref[m, here, :], resid_ref[m, here, :]], axis=1)
        for first in range(0, lats, strip):
            cols = slice(first, first + strip)
            total = jnp.dot(left, right_ref[:, cols], preferred_element_type=F32)
            held_ref[i % slots, :, cols] = (scale * total).astype(BF16)
        copies.append(
            pltpu.make_async_copy(held_ref.at[i % slots], out_ref.at[m, here], sems.at[i % slots])
        )
        copies[i].start()
    for copy in copies[-slots:]:
        copy.wait()


def grad_weights(scale, acts, resid, own, others, slopes, latents):
    models, width, rows = acts.shape
    lats = latents[0].shape[1]
    block = min(width, 512)
    groups, slots = len(own), 8
    return call(
        functools.partial(grad_kernel, scale, groups, slots),
        (
            jax.ShapeDtypeStruct((models, width, lats), BF16),
            jax.ShapeDtypeStruct((1, lats), F32),
        ),
        (acts, resid, *own, *others, *slopes, *latents),
        flops=4 * models * rows * width * lats,
        moved=2 * models * width * lats,
        limit=24 * MIB,
        in_specs=[WHOLE] * (2 + 4 * groups),
        out_specs=(pl.BlockSpec(memory_space=pltpu.HBM), WHOLE),
        scratch_shapes=[
            pltpu.VMEM((2 * rows, lats), BF16),
            pltpu.VMEM((slots, block, lats), BF16),
            pltpu.SemaphoreType.DMA((slots,)),
        ],
        name="grad_weights",
    )


def along(x, size, rest, own):
    for stage in rest[::-1]:
        others = [shift(x, size, stage, step) for step in range(1, stage[1])]
        x = own = jnp.concatenate([own] + others, axis=1)
    return own


def gather_direct(x, size, own, work):
    core, group, rest = stages(size)
    pieces, done = [], []
    first = [x] + [shift(x, size, group, step) for step in range(1, group[1])]
    for k, part in enumerate(first):
        block = along(part, size, rest, part if k else own)
        piece = [block] + [shift(block, size, core, step) for step in range(1, core[1])]
        pieces.append(piece)
        done.append(work(piece))
    return pieces, done


def sum_group(keep, sends, size):
    core, _, rest = stages(size)
    total = keep
    for step in range(1, core[1]):
        total = total + shift(sends[step - 1], size, core, step).astype(F32)
    for stage in rest:
        radix = stage[1]
        rows = total.shape[1] // radix
        parts = [total[:, k * rows:(k + 1) * rows] for k in range(radix)]
        total = parts[0]
        for step in range(1, radix):
            sent = parts[step].astype(BF16)
            total = total + shift(sent, size, stage, step).astype(F32)
    return total


def on_device(acts, weight, enc_bias, dec_bias):
    n_feat, n_lat = lax.axis_size("feat"), lax.axis_size("lat")
    core, group, _ = stages(n_lat)
    n_group = group[1]
    scale = math.sqrt(2.0 * weight.shape[1] * n_feat / (weight.shape[2] * n_lat))
    whole, own = gather_direct(acts, n_lat, hold(acts), lambda x: times_weight(x, weight))
    turned = turn_weight(weight)
    got = []
    for x in own:
        got.append(feat_others(x, n_feat))
    latents, sums = [], []
    for x, others in zip(own, got):
        lat, keep, *sends = decode(x, others, enc_bias[None, :], turned, core[1])
        latents.append(lat)
        sums.append(sum_group(keep, sends, n_lat))
    slopes = [jax.nn.sigmoid(add_terms(x, y) + enc_bias) for x, y in zip(own, got)]
    recon = sums[0]
    for step in range(1, n_group):
        sent = sums[step].astype(BF16)
        recon = recon + shift(sent, n_lat, group, step).astype(F32)
    resid = (scale * recon + dec_bias[:, None, :] - acts.astype(F32)).astype(BF16)
    resid_rows, back = gather_direct(resid, n_lat, resid, lambda x: times_weight(x, weight))
    others = []
    for x in back:
        others.append(jnp.stack(feat_others(x, n_feat)))
    flat_acts = [x for pieces in whole for x in pieces]
    flat_resid = [x for pieces in resid_rows for x in pieces]
    grad_dec_bias = sum(jnp.sum(x.astype(F32), axis=1) for x in flat_resid)
    grad_weight, grad_enc_bias = grad_weights(
        scale, turn(flat_acts), turn(flat_resid), back, others, slopes, latents
    )
    return (grad_weight, grad_enc_bias.reshape(-1), grad_dec_bias)


def solution(mesh):
    placed = (P(None, "lat", "feat"), P(None, "feat", "lat"), P("lat"), P(None, "feat"))
    return jax.shard_map(
        on_device,
        mesh=mesh,
        in_specs=placed,
        out_specs=(P(None, "feat", "lat"), P("lat"), P(None, "feat")),
        check_vma=False,
    )
```
